32 devices in a mesh: dom: 8 (over z, y), sub: 4 (over x, core).
Axes of the slice: x: 2, y: 2, z: 4, core: 2. Of those that a mesh axis runs over, the one named last changes fastest.
Arguments:
- nodes: bfloat16 [16384, 128], P(('dom', 'sub')), may hold values from -6 to 6
- edges: bfloat16 [65536, 128], P(('dom', 'sub')), may hold values from -6 to 6
- senders: int32 [65536], P(('dom', 'sub')), may hold values from 0 to 895
- receivers: int32 [65536], P(('dom', 'sub')), may hold values from 0 to 511
- edge_live: int32 [65536], P(('dom', 'sub')), may hold values from 0 to 1, as said below
- outlet_flags: int32 [16384], P(('dom', 'sub')), may hold values 0 or 1
- send_rows: int32 [12288], P(('dom', 'sub')), may hold values from 0 to 511
- edge_first: float32 [3, 384, 128], replicated, may hold values from -0.3125 to 0.3125
- edge_bias: float32 [3, 128], replicated, may hold values from -3 to 3
- edge_second: float32 [3, 128, 128], replicated, may hold values from -0.5 to 0.5
- edge_offset: float32 [3, 128], replicated, may hold values from -3 to 3
- edge_gain: float32 [3, 128], replicated, may hold values from 0.25 to 1.75
- node_first: float32 [3, 256, 128], replicated, may hold values from -0.375 to 0.375
- node_bias: float32 [3, 128], replicated, may hold values from -3 to 3
- node_second: float32 [3, 128, 128], replicated, may hold values from -0.5 to 0.5
- node_offset: float32 [3, 128], replicated, may hold values from -3 to 3
- node_gain: float32 [3, 128], replicated, may hold values from 0.25 to 1.75
- outlet_map: float32 [3, 128, 128], replicated, may hold values from -0.5 to 0.5
- grad_out: float32 [16384, 128], P(('dom', 'sub')), may hold values from -6 to 6
Outputs:
- latent_out: float32 [16384, 128], P(('dom', 'sub'))
- latent_grad: float32 [16384, 128], P(('dom', 'sub'))
- edge_first_grad: float32 [3, 384, 128], replicated
- edge_bias_grad: float32 [3, 128], replicated
- edge_second_grad: float32 [3, 128, 128], replicated
- edge_offset_grad: float32 [3, 128], replicated
- edge_gain_grad: float32 [3, 128], replicated
- node_first_grad: float32 [3, 256, 128], replicated
- node_bias_grad: float32 [3, 128], replicated
- node_second_grad: float32 [3, 128, 128], replicated
- node_offset_grad: float32 [3, 128], replicated
- node_gain_grad: float32 [3, 128], replicated
- outlet_map_grad: float32 [3, 128, 128], replicated
The draws below stay inside these ranges and needn't reach their ends.
Inputs may be any that keep to these rules, and one draw needn't show every extreme that they name: `edge_live`: on each device the live edge slots are the first ones of its 2048; each device has between a quarter and all of them live, and some device has all live. `senders`: indices below 512 name the device's own nodes; higher ones name halo rows.
All inputs are finite; a program needn't handle non-finite values. No bound on the sum of `outlet_flags` on one device may be relied on, other than what follows from the above.
Results may differ from the reference program's by a relative error of at most 0.018.
Values may be sent and summed in bfloat16 or wider, within the bound.
A program may use at most 320 MiB of HBM per device.

```python
import jax
import jax.numpy as jnp
from jax import lax

D = 128
HID = 128
LAYERS = 3
NODE_DEV = 512
EDGE_DEV = 2048
SIDE_SUB = 64
SIDE_DOM = 128
SEND_DEV = 384
NODES = 16384
EDGES = 65536
N_DOM = 8
N_SUB = 4


def draw_edge_live(key, part):
    count_key, pick_key = jax.random.split(jax.random.fold_in(key, 17))
    devices = EDGES // EDGE_DEV
    counts = jax.random.randint(count_key, (devices,), EDGE_DEV // 4, EDGE_DEV + 1)
    chosen = jax.random.randint(pick_key, (), 0, devices)
    counts = jnp.where(jnp.arange(devices) == chosen, EDGE_DEV, counts)
    live = jnp.arange(EDGE_DEV)[None, :] < counts[:, None]
    return live.astype(jnp.int32).reshape(EDGES)


def set_ends(entries, rng, low, largest):
    longest = entries.shape.index(max(entries.shape))
    spots = []
    for shift in (0, 1):
        where = [jax.random.randint(jax.random.fold_in(rng, axis), (), 0, length) for axis, length in enumerate(entries.shape)]
        where[longest] = (where[longest] + shift) % entries.shape[longest]
        spots.append(tuple(where))
    return entries.at[spots[0]].set(low).at[spots[1]].set(largest)


def block_scale(own_key, shape, pieces, low, high):
    loudness, own = 1.0, jax.random.fold_in(own_key, 6)
    for dim, parts in pieces:
        steps = jnp.exp(jax.random.uniform(jax.random.fold_in(own, dim), (parts,), jnp.float32, low / len(pieces), high / len(pieces)))
        loudness = loudness * jnp.repeat(steps, shape[dim] // parts).reshape([-1 if axis == dim else 1 for axis in range(len(shape))])
    return loudness


def normal_values(stream_key, shape, scale, limit, cuts=(), dtype=jnp.bfloat16):
    result = scale * jax.random.normal(stream_key, shape, jnp.float32)
    if cuts:
        result = result * block_scale(stream_key, shape, cuts, -0.22, 0.18)
    return jnp.clip(result, -limit, limit).astype(dtype)


def setup_inputs(seed: int = 0) -> dict:
    arg_keys = jax.random.split(jax.random.key(seed), 20)
    return {
        "nodes": normal_values(arg_keys[0], (NODES, D), 1.0, 6.0, ((0, 32),)),
        "edges": normal_values(arg_keys[1], (EDGES, D), 1.0, 6.0, ((0, 32),)),
        "senders": set_ends(jax.random.randint(arg_keys[2], (EDGES,), 0, NODE_DEV + SEND_DEV), jax.random.fold_in(arg_keys[2], 1), 0, (NODE_DEV + SEND_DEV) - 1).astype(jnp.int32),
        "receivers": set_ends(jax.random.randint(arg_keys[3], (EDGES,), 0, NODE_DEV), jax.random.fold_in(arg_keys[3], 1), 0, NODE_DEV - 1).astype(jnp.int32),
        "edge_live": draw_edge_live(jax.random.fold_in(arg_keys[19], 71), 0),
        "outlet_flags": set_ends((jax.random.randint(arg_keys[5], (NODES,), 0, 8) < 1).astype(jnp.int32), jax.random.fold_in(arg_keys[5], 1), 0, 1),
        "send_rows": set_ends(jax.random.randint(arg_keys[6], (N_DOM * N_SUB * SEND_DEV,), 0, NODE_DEV), jax.random.fold_in(arg_keys[6], 1), 0, NODE_DEV - 1).astype(jnp.int32),
        "edge_first": normal_values(arg_keys[7], (LAYERS, 3 * D, HID), (3 * D) ** -0.5, 0.3125, (), jnp.float32),
        "edge_bias": normal_values(arg_keys[8], (LAYERS, HID), 0.5, 3.0, (), jnp.float32),
        "edge_second": normal_values(arg_keys[9], (LAYERS, HID, D), HID ** -0.5, 0.5, (), jnp.float32),
        "edge_offset": normal_values(arg_keys[10], (LAYERS, D), 0.5, 3.0, (), jnp.float32),
        "edge_gain": jnp.clip(1.0 + 0.15 * jax.random.normal(arg_keys[11], (LAYERS, D), jnp.float32), 0.25, 1.75),
        "node_first": normal_values(arg_keys[12], (LAYERS, 2 * D, HID), (2 * D) ** -0.5, 0.375, (), jnp.float32),
        "node_bias": normal_values(arg_keys[13], (LAYERS, HID), 0.5, 3.0, (), jnp.float32),
        "node_second": normal_values(arg_keys[14], (LAYERS, HID, D), HID ** -0.5, 0.5, (), jnp.float32),
        "node_offset": normal_values(arg_keys[15], (LAYERS, D), 0.5, 3.0, (), jnp.float32),
        "node_gain": jnp.clip(1.0 + 0.15 * jax.random.normal(arg_keys[16], (LAYERS, D), jnp.float32), 0.25, 1.75),
        "outlet_map": normal_values(arg_keys[17], (LAYERS, D, D), D ** -0.5, 0.5, (), jnp.float32),
        "grad_out": normal_values(arg_keys[18], (NODES, D), 1.0, 6.0, ((0, 32),), jnp.float32),
    }


def normalize(values):
    mean = lax.optimization_barrier(jnp.mean(values, axis=-1, keepdims=True))
    centered = values - mean
    variance = lax.optimization_barrier(jnp.mean(centered * centered, axis=-1, keepdims=True))
    return centered * lax.rsqrt(variance + 1e-05)

def layer_local(latent, edge_state, halo, layer_weights, senders, receivers, live, flags):
    edge_first, edge_bias, edge_second, edge_offset, edge_gain, node_first, node_bias, node_second, node_offset, node_gain, outlet_map = layer_weights
    own = latent.astype(jnp.bfloat16)
    extended = jnp.concatenate([own, halo], axis=0)
    joined = jnp.concatenate([edge_state.astype(jnp.bfloat16), extended[senders], own[receivers]], axis=1)
    act_one = jax.nn.silu(jnp.dot(joined, edge_first.astype(jnp.bfloat16), preferred_element_type=jnp.float32) + edge_bias).astype(jnp.bfloat16)
    pre_two = jnp.dot(act_one, edge_second.astype(jnp.bfloat16), preferred_element_type=jnp.float32) + edge_offset
    message = live[:, None] * (edge_gain * normalize(pre_two))
    new_edge = edge_state + message
    summed = jax.ops.segment_sum(message, receivers, num_segments=latent.shape[0])
    summed_half = summed.astype(jnp.bfloat16)
    node_in = jnp.concatenate([own, summed_half], axis=1)
    node_hidden = jax.nn.silu(jnp.dot(node_in, node_first.astype(jnp.bfloat16), preferred_element_type=jnp.float32) + node_bias).astype(jnp.bfloat16)
    update = node_gain * normalize(jnp.dot(node_hidden, node_second.astype(jnp.bfloat16), preferred_element_type=jnp.float32) + node_offset)
    outlet = flags[:, None] * jnp.dot(summed_half, outlet_map.astype(jnp.bfloat16), preferred_element_type=jnp.float32)
    return (latent + update + outlet, new_edge)

def exchange_rows(latent, send):
    count = N_DOM * N_SUB
    low = SIDE_SUB
    high = SIDE_DOM
    sent = jax.vmap(lambda rows, picks: rows[picks])(latent, send).astype(jnp.bfloat16)
    grid = sent.reshape(N_DOM, N_SUB, SEND_DEV, D)
    zero_sub = jnp.zeros((N_DOM, 1, low, D), jnp.bfloat16)
    zero_dom = jnp.zeros((1, N_SUB, high, D), jnp.bfloat16)
    from_lower = jnp.concatenate([zero_sub, grid[:, :-1, low:2 * low]], axis=1)
    from_upper = jnp.concatenate([grid[:, 1:, :low], zero_sub], axis=1)
    dom_lower = jnp.concatenate([zero_dom, grid[:-1, :, 2 * low + high:]], axis=0)
    dom_upper = jnp.concatenate([grid[1:, :, 2 * low:2 * low + high], zero_dom], axis=0)
    halo = jnp.concatenate([from_lower, from_upper, dom_lower, dom_upper], axis=2)
    return halo.reshape(count, SEND_DEV, D)

def reference(nodes, edges, senders, receivers, edge_live, outlet_flags, send_rows, edge_first, edge_bias, edge_second, edge_offset, edge_gain, node_first, node_bias, node_second, node_offset, node_gain, outlet_map, grad_out):
    count = N_DOM * N_SUB
    latent_start = nodes.astype(jnp.float32).reshape(count, NODE_DEV, D)
    edge_start = edges.astype(jnp.float32).reshape(count, EDGE_DEV, D)
    send = send_rows.reshape(count, SEND_DEV)
    sender_idx = senders.reshape(count, EDGE_DEV)
    receiver_idx = receivers.reshape(count, EDGE_DEV)
    live = edge_live.astype(jnp.float32).reshape(count, EDGE_DEV)
    flags = outlet_flags.astype(jnp.float32).reshape(count, NODE_DEV)
    weights = (edge_first, edge_bias, edge_second, edge_offset, edge_gain, node_first, node_bias, node_second, node_offset, node_gain, outlet_map)
    copies = tuple((jnp.broadcast_to(weight[None], (count,) + weight.shape) for weight in weights))

    def one_layer(latent, edge_state, layer_copies):
        halo = exchange_rows(latent, send)
        return jax.vmap(layer_local)(latent, edge_state, halo, layer_copies, sender_idx, receiver_idx, live, flags)
    checked = jax.checkpoint(one_layer)

    def forward(latent, all_copies):
        edge_state = edge_start
        for layer in range(LAYERS):
            latent, edge_state = checked(latent, edge_state, tuple((copy[:, layer] for copy in all_copies)))
        return latent
    final, pullback = jax.vjp(forward, latent_start, copies)
    latent_grad, copy_grads = pullback(grad_out.reshape(count, NODE_DEV, D))
    summed = tuple((lax.optimization_barrier(jnp.sum(grad, axis=0)) for grad in copy_grads))
    g_ef, g_eb, g_es, g_eo, g_eg, g_nf, g_nb, g_ns, g_no, g_ng, g_om = summed
    return (final.reshape(NODES, D), latent_grad.reshape(NODES, D), g_ef, g_eb, g_es, g_eo, g_eg, g_nf, g_nb, g_ns, g_no, g_ng, g_om)
```

```python
import functools

import jax
import jax.numpy as jnp
from jax import lax
from jax.experimental import pallas as pl
from jax.experimental.pallas import tpu as pltpu
from jax.sharding import PartitionSpec as P

F32 = jnp.float32
BF16 = jnp.bfloat16
EPS = 1e-05


def mm(a, b):
    return jnp.dot(a, b, preferred_element_type=F32)


def mm_tn(a, b):
    return lax.dot_general(a, b, (((0,), (0,)), ((), ())), preferred_element_type=F32)


def mm_nt(a, b):
    return lax.dot_general(a, b, (((1,), (1,)), ((), ())), preferred_element_type=F32)


def rsum(v):
    return jnp.sum(v, axis=0, keepdims=True)


def lmean(v):
    return jnp.mean(v, axis=-1, keepdims=True)


def remote(src, dst, send_sem, recv_sem, device):
    return pltpu.make_async_remote_copy(
        src_ref=src,
        dst_ref=dst,
        send_sem=send_sem,
        recv_sem=recv_sem,
        device_id=device,
        device_id_type=pl.DeviceIdType.MESH,
    )


def as_column(row):
    width = row.shape[1]
    eye = lax.broadcasted_iota(jnp.int32, (width, width), 0) == lax.broadcasted_iota(
        jnp.int32, (width, width), 1
    )
    return jnp.sum(jnp.where(eye, row.astype(F32), 0.0), axis=1, keepdims=True)


def silu_parts(x):
    sig = 0.5 * jnp.tanh(0.5 * x) + 0.5
    return x * sig, sig * (1.0 + x * (1.0 - sig))


def kernel(dims, *refs):
    nd, ns, layers, n, e, sr, D, te, r2 = dims
    (nodes, edges, snd, rcv, live, flags, send,
     w1, b1, w2, o1, g1, wn, nb, wn2, no, ng, wo, gout,
     out_l, out_g, q_w1, q_b1, q_w2, q_o1, q_g1, q_wn, q_nb, q_wn2, q_no, q_ng, q_wo,
     ohs, ohst, ohr, ohrt, ohx, ohxt, fcol,
     c_w1, c_w2, c_wn, c_wn2, c_wo,
     joined, act, ds1, xhat, rstd, estate, summed,
     nin, hid, dsn, nxhat, nrstd, lat,
     sent, halo, hgrad, ret,
     dedge, dp1, dp2, dext, dsh, glat, acc1, acc2, bacc,
     flat, r1, f2, rr2, g3, g4, br1, bs1, br2,
     hs_s, hs_r, hb_s, hb_r, q1s, q1r, q2s, q2r, q3s, q3r, q4s, q4r, bq1s, bq1r, bq2s, bq2r,
     ) = refs
    d = lax.axis_index("dom")
    s = lax.axis_index("sub")
    low, high = sr // 6, sr // 3
    c1 = nd * r2
    tiles = e // te
    hid_rows = w2.shape[1]
    k1 = w1.shape[1]
    kn = wn.shape[1]

    halo[...] = jnp.zeros_like(halo)
    ret[...] = jnp.zeros_like(ret)

    barrier = pltpu.get_barrier_semaphore()
    for k in range(1, ns):
        pl.semaphore_signal(barrier, inc=1, device_id=(d, lax.rem(s + k, ns)),
                            device_id_type=pl.DeviceIdType.MESH)
    for k in range(1, nd):
        pl.semaphore_signal(barrier, inc=1, device_id=(lax.rem(d + k, nd), s),
                            device_id_type=pl.DeviceIdType.MESH)
    pl.semaphore_wait(barrier, ns - 1 + nd - 1)

    S_rows = [(low, low), (0, low), (2 * low + high, high), (2 * low, high)]
    H_rows = [(0, low), (low, low), (2 * low, high), (2 * low + high, high)]
    has_next = [s < ns - 1, s > 0, d < nd - 1, d > 0]
    has_prev = [s > 0, s < ns - 1, d > 0, d < nd - 1]
    nxt = [(d, jnp.minimum(s + 1, ns - 1)), (d, jnp.maximum(s - 1, 0)),
           (jnp.minimum(d + 1, nd - 1), s), (jnp.maximum(d - 1, 0), s)]
    prv = [nxt[1], nxt[0], nxt[3], nxt[2]]

    def part(ref, layer, rows):
        return ref.at[layer, pl.ds(rows[0], rows[1])]

    def halo_copy(layer, i):
        return remote(part(sent, layer, S_rows[i]), part(halo, layer, H_rows[i]),
                      hs_s.at[layer, i], hs_r.at[layer, i], nxt[i])

    def back_copy(layer, i):
        return remote(part(hgrad, layer, H_rows[i]), part(ret, layer, S_rows[i]),
                      hb_s.at[layer, i], hb_r.at[layer, i], prv[i])

    def start_moves(make, layer, sends):
        for i in range(4):
            @pl.when(sends[i])
            def _(i=i):
                make(layer, i).start()

    def wait_moves(make, layer, sends, recvs):
        for i in range(4):
            @pl.when(recvs[i])
            def _(i=i):
                make(layer, i).wait_recv()
        for i in range(4):
            @pl.when(sends[i])
            def _(i=i):
                make(layer, i).wait_send()

    def build(ids, count, oh, oht, mask):
        width = oh.shape[1]

        def body(r, carry):
            row = ids[pl.ds(r, 1), :]
            if mask is not None:
                row = jnp.where(mask[pl.ds(r, 1), :] > 0, row, -1)
            at = pl.multiple_of(r * 128, 128)
            down = lax.broadcasted_iota(jnp.int32, (width, 128), 0)
            oht[:, pl.ds(at, 128)] = jnp.where(down == row, 1.0, 0.0).astype(BF16)
            col = as_column(row).astype(jnp.int32)
            across = lax.broadcasted_iota(jnp.int32, (128, width), 1)
            oh[pl.ds(at, 128), :] = jnp.where(across == col, 1.0, 0.0).astype(BF16)
            return carry

        lax.fori_loop(0, count // 128, body, 0)

    build(send, sr, ohx, ohxt, None)

    lat[...] = nodes[...].astype(F32)

    def start_layer(layer):
        own = lat[...].astype(BF16)
        nin[layer, :, 0:D] = own
        sent[layer] = mm(ohx[...], own).astype(BF16)
        start_moves(halo_copy, layer, has_next)

    start_layer(0)
    build(snd, e, ohs, ohst, None)
    build(rcv, e, ohr, ohrt, live)

    def flag_body(r, carry):
        at = pl.multiple_of(r * 128, 128)
        fcol[pl.ds(at, 128), :] = as_column(flags[pl.ds(r, 1), :])
        return carry

    lax.fori_loop(0, n // 128, flag_body, 0)
    for layer in range(layers):
        c_w1[layer] = w1[layer].astype(BF16)
        c_w2[layer] = w2[layer].astype(BF16)
        c_wn[layer] = wn[layer].astype(BF16)
        c_wn2[layer] = wn2[layer].astype(BF16)
        c_wo[layer] = wo[layer].astype(BF16)
    bacc[...] = jnp.zeros_like(bacc)
    estate[...] = edges[...].astype(F32)
    pad = flat.shape[1] - (k1 + hid_rows + kn + 2 * D)
    if pad:
        for layer in range(layers):
            flat[layer, pl.ds(k1 + hid_rows + kn + 2 * D, pad), :] = jnp.zeros((pad, D), BF16)

    for layer in range(layers):
        own = nin[layer, :, 0:D]

        def local(t, carry, layer=layer):
            rows = pl.ds(pl.multiple_of(t * te, te), te)
            own = nin[layer, :, 0:D]
            joined[layer, rows, 0:D] = estate[rows, :].astype(BF16)
            joined[layer, rows, D:2 * D] = mm(ohs[rows, 0:n], own).astype(BF16)
            joined[layer, rows, 2 * D:3 * D] = mm(ohr[rows, :], own).astype(BF16)
            return carry

        lax.fori_loop(0, tiles, local, 0)
        summed[...] = jnp.zeros_like(summed)
        wait_moves(halo_copy, layer, has_next, has_prev)

        def edge(t, carry, layer=layer):
            rows = pl.ds(pl.multiple_of(t * te, te), te)
            far = mm(ohs[rows, n:], halo[layer])
            xs = (joined[layer, rows, D:2 * D].astype(F32) + far).astype(BF16)
            joined[layer, rows, D:2 * D] = xs
            pre = mm(joined[layer, rows, :], c_w1[layer]) + b1[pl.ds(layer, 1), :]
            a, da = silu_parts(pre)
            a = a.astype(BF16)
            act[layer, rows, :] = a
            ds1[layer, rows, :] = da
            two = mm(a, c_w2[layer]) + o1[pl.ds(layer, 1), :]
            cen = two - lmean(two)
            rs = lax.rsqrt(lmean(cen * cen) + EPS)
            xh = cen * rs
            xhat[layer, rows, :] = xh
            rstd[layer, rows, :] = rs
            msg = g1[pl.ds(layer, 1), :] * xh
            estate[rows, :] += msg
            summed[...] += mm(ohrt[:, rows], msg.astype(BF16))
            return carry

        lax.fori_loop(0, tiles, edge, 0)

        sh = summed[...].astype(BF16)
        nin[layer, :, D:2 * D] = sh
        pre = mm(nin[layer], c_wn[layer]) + nb[pl.ds(layer, 1), :]
        a, da = silu_parts(pre)
        a = a.astype(BF16)
        hid[layer] = a
        dsn[layer] = da
        two = mm(a, c_wn2[layer]) + no[pl.ds(layer, 1), :]
        cen = two - lmean(two)
        rs = lax.rsqrt(lmean(cen * cen) + EPS)
        xh = cen * rs
        nxhat[layer] = xh
        nrstd[layer] = rs
        lat[...] = lat[...] + ng[pl.ds(layer, 1), :] * xh + fcol[...] * mm(sh, c_wo[layer])
        if layer + 1 < layers:
            start_layer(layer + 1)
    out_l[...] = lat[...]

    def s1(layer, k):
        peer = lax.rem(s + k, ns)
        return remote(flat.at[layer, pl.ds(pl.multiple_of(peer * c1, 16), c1)], r1.at[layer, s],
                      q1s.at[layer, k], q1r.at[layer, k], (d, peer))

    def s2(layer, k):
        peer = lax.rem(d + k, nd)
        return remote(f2.at[layer, pl.ds(pl.multiple_of(peer * r2, 16), r2)], rr2.at[layer, d],
                      q2s.at[layer, k], q2r.at[layer, k], (peer, s))

    def s3(layer, k):
        peer = lax.rem(d + k, nd)
        mine = g3.at[layer, pl.ds(pl.multiple_of(d * r2, 16), r2)]
        return remote(mine, mine, q3s.at[layer, k], q3r.at[layer, k], (peer, s))

    def s4(layer, k):
        peer = lax.rem(s + k, ns)
        return remote(g3.at[layer], g4.at[layer, pl.ds(pl.multiple_of(s * c1, 16), c1)],
                      q4s.at[layer, k], q4r.at[layer, k], (d, peer))

    def bias1(layer, k):
        return remote(bacc, br1.at[s], bq1s.at[k], bq1r.at[k], (d, lax.rem(s + k, ns)))

    def bias2(layer, k):
        return remote(bs1, br2.at[d], bq2s.at[k], bq2r.at[k], (lax.rem(d + k, nd), s))

    def start_all(make, layer, count):
        for k in range(1, count):
            make(layer, k).start()

    def wait_all(make, layer, count):
        for k in range(1, count):
            make(layer, k).wait_recv()
        for k in range(1, count):
            make(layer, k).wait_send()

    def stage1(layer):
        start_all(s1, layer, ns)

    def stage2(layer):
        r1[layer, s] = flat[layer, pl.ds(pl.multiple_of(s * c1, 16), c1), :]
        wait_all(s1, layer, ns)
        total = r1[layer, 0].astype(F32)
        for j in range(1, ns):
            total = total + r1[layer, j].astype(F32)
        f2[layer] = total.astype(BF16)
        start_all(s2, layer, nd)

    def stage3(layer):
        rr2[layer, d] = f2[layer, pl.ds(pl.multiple_of(d * r2, 16), r2), :]
        wait_all(s2, layer, nd)
        total = rr2[layer, 0].astype(F32)
        for j in range(1, nd):
            total = total + rr2[layer, j].astype(F32)
        g3[layer, pl.ds(pl.multiple_of(d * r2, 16), r2), :] = total.astype(BF16)
        start_all(s3, layer, nd)

    def stage4(layer):
        wait_all(s3, layer, nd)
        start_all(s4, layer, ns)
        g4[layer, pl.ds(pl.multiple_of(s * c1, 16), c1), :] = g3[layer]

    def stage5(layer):
        wait_all(s4, layer, ns)
        at = 0
        for out, count in ((q_w1, k1), (q_w2, hid_rows), (q_wn, kn), (q_wn2, D), (q_wo, D)):
            out[layer] = g4[layer, pl.ds(at, count), :].astype(F32)
            at += count

    def norm_back(dxh, xh, rs):
        return rs * (dxh - lmean(dxh) - xh * lmean(dxh * xh))

    glat[...] = gout[...]
    dedge[...] = jnp.zeros_like(dedge)
    for layer in reversed(range(layers)):
        row = layer * 6
        g = glat[...]
        xh = nxhat[layer]
        bacc[pl.ds(row + 5, 1), :] = rsum(g * xh)
        dtwo = norm_back(g * ng[pl.ds(layer, 1), :], xh, nrstd[layer])
        bacc[pl.ds(row + 4, 1), :] = rsum(dtwo)
        dtwo = dtwo.astype(BF16)
        dh = mm_nt(dtwo, c_wn2[layer]).astype(BF16).astype(F32)
        dpre = dh * dsn[layer]
        bacc[pl.ds(row + 3, 1), :] = rsum(dpre)
        dpre = dpre.astype(BF16)
        dout = (fcol[...] * g).astype(BF16)
        dnin = mm_nt(dpre, c_wn[layer])
        dsum = dnin[:, D:].astype(BF16).astype(F32) + mm_nt(dout, c_wo[layer]).astype(BF16).astype(F32)
        dsh[...] = dsum.astype(BF16)
        dext[...] = jnp.zeros_like(dext)
        glat[...] = g + dnin[:, :D]

        def edge_back(t, carry, layer=layer, row=row):
            rows = pl.ds(pl.multiple_of(t * te, te), te)
            dmsg = dedge[rows, :] + mm(ohr[rows, :], dsh[...])
            xh = xhat[layer, rows, :]
            bacc[pl.ds(row + 2, 1), :] += rsum(dmsg * xh)
            dtwo = norm_back(dmsg * g1[pl.ds(layer, 1), :], xh, rstd[layer, rows, :])
            bacc[pl.ds(row + 1, 1), :] += rsum(dtwo)
            dtwo = dtwo.astype(BF16)
            dp2[rows, :] = dtwo
            da = mm_nt(dtwo, c_w2[layer]).astype(BF16).astype(F32)
            dpre = da * ds1[layer, rows, :]
            bacc[pl.ds(row, 1), :] += rsum(dpre)
            dpre = dpre.astype(BF16)
            dp1[rows, :] = dpre
            dj = mm_nt(dpre, c_w1[layer]).astype(BF16)
            dext[...] += mm(ohst[:, rows], dj[:, D:2 * D])
            glat[...] += mm(ohrt[:, rows], dj[:, 2 * D:])
            if layer > 0:
                dedge[rows, :] += dj[:, 0:D].astype(F32)
            return carry

        lax.fori_loop(0, tiles, edge_back, 0)
        hgrad[layer] = dext[n:, :].astype(BF16)
        start_moves(back_copy, layer, has_prev)

        acc1[...] = jnp.zeros_like(acc1)
        acc2[...] = jnp.zeros_like(acc2)

        def grads(t, carry, layer=layer):
            rows = pl.ds(pl.multiple_of(t * te, te), te)
            acc1[...] += mm_tn(joined[layer, rows, :], dp1[rows, :])
            acc2[...] += mm_tn(act[layer, rows, :], dp2[rows, :])
            return carry

        lax.fori_loop(0, tiles, grads, 0)
        at = 0
        for value in (acc1[...], acc2[...], mm_tn(nin[layer], dpre),
                      mm_tn(hid[layer], dtwo), mm_tn(nin[layer, :, D:2 * D], dout)):
            count = value.shape[0]
            flat[layer, pl.ds(at, count), :] = value.astype(BF16)
            at += count
        stage1(layer)
        if layer == 0:
            start_all(bias1, 0, ns)
        if layer + 1 < layers:
            stage2(layer + 1)
        if layer + 2 < layers:
            stage4(layer + 2)
        glat[...] += dext[0:n, :]
        wait_moves(back_copy, layer, has_prev, has_next)
        glat[...] += mm(ohxt[...], ret[layer])
        if layer + 1 < layers:
            stage3(layer + 1)
        if layer + 2 < layers:
            stage5(layer + 2)
    out_g[...] = glat[...]

    stage2(0)
    br1[s] = bacc[...]
    wait_all(bias1, 0, ns)
    total = br1[0]
    for j in range(1, ns):
        total = total + br1[j]
    bs1[...] = total
    start_all(bias2, 0, nd)
    if layers > 1:
        stage4(1)
    stage3(0)
    br2[d] = bs1[...]
    wait_all(bias2, 0, nd)
    total = br2[0]
    for j in range(1, nd):
        total = total + br2[j]
    for layer in range(layers):
        for i, out in enumerate((q_b1, q_o1, q_g1, q_nb, q_no, q_ng)):
            out[pl.ds(layer, 1), :] = total[layer * 6 + i:layer * 6 + i + 1, :]
    stage4(0)
    if layers > 1:
        stage5(1)
    stage5(0)


def on_device(nd, ns, nodes, edges, senders, receivers, edge_live, outlet_flags, send_rows, *rest):
    weights, grad_out = rest[:-1], rest[-1]
    n, D = nodes.shape
    e = edges.shape[0]
    sr = send_rows.shape[0]
    layers = weights[0].shape[0]
    te = min(512, e)
    grad_rows = sum(w.shape[1] for w in weights if w.ndim == 3)
    r2 = pl.cdiv(grad_rows, ns * nd * 16) * 16
    c1 = nd * r2
    total = ns * c1
    brows = pl.cdiv(6 * layers, 8) * 8
    ext = n + sr
    dims = (nd, ns, layers, n, e, sr, D, te, r2)
    V = pltpu.VMEM
    scratch = [
        V((e, ext), BF16), V((ext, e), BF16), V((e, n), BF16), V((n, e), BF16),
        V((sr, n), BF16), V((n, sr), BF16), V((n, 1), F32),
        V(weights[0].shape, BF16), V(weights[2].shape, BF16), V(weights[5].shape, BF16),
        V(weights[7].shape, BF16), V(weights[10].shape, BF16),
        V((layers, e, 3 * D), BF16), V((layers, e, D), BF16), V((layers, e, D), F32),
        V((layers, e, D), F32), V((layers, e, 1), F32), V((e, D), F32), V((n, D), F32),
        V((layers, n, 2 * D), BF16), V((layers, n, D), BF16), V((layers, n, D), F32),
        V((layers, n, D), F32), V((layers, n, 1), F32), V((n, D), F32),
        V((layers, sr, D), BF16), V((layers, sr, D), BF16), V((layers, sr, D), BF16),
        V((layers, sr, D), BF16),
        V((e, D), F32), V((e, D), BF16), V((e, D), BF16), V((ext, D), F32), V((n, D), BF16),
        V((n, D), F32), V((3 * D, D), F32), V((D, D), F32), V((brows, D), F32),
        V((layers, total, D), BF16), V((layers, ns, c1, D), BF16), V((layers, c1, D), BF16),
        V((layers, nd, r2, D), BF16), V((layers, c1, D), BF16), V((layers, total, D), BF16),
        V((ns, brows, D), F32), V((brows, D), F32), V((nd, brows, D), F32),
    ]
    sem = pltpu.SemaphoreType.DMA
    scratch += [sem((layers, 4))] * 4
    scratch += [sem((layers, ns))] * 2 + [sem((layers, nd))] * 4 + [sem((layers, ns))] * 2
    scratch += [sem((ns,))] * 2 + [sem((nd,))] * 2
    shapes = [jax.ShapeDtypeStruct((n, D), F32)] * 2 + [
        jax.ShapeDtypeStruct(w.shape, F32) for w in weights
    ]
    vmem = pl.BlockSpec(memory_space=pltpu.VMEM)
    rows = lambda v: v.reshape(-1, 128)
    args = (nodes, edges, rows(senders), rows(receivers), rows(edge_live), rows(outlet_flags),
            rows(send_rows), *weights, grad_out)
    return tuple(pl.pallas_call(
        functools.partial(kernel, dims),
        out_shape=shapes,
        in_specs=[vmem] * len(args),
        out_specs=[vmem] * len(shapes),
        scratch_shapes=scratch,
        compiler_params=pltpu.CompilerParams(
            collective_id=0, has_side_effects=True, vmem_limit_bytes=60 * 1024 * 1024
        ),
    )(*args))


def solution(mesh):
    split = ("dom", "sub")
    placed = (P(split, None),) * 2 + (P(split),) * 5 + (P(),) * 11 + (P(split, None),)
    return jax.shard_map(
        functools.partial(on_device, mesh.shape["dom"], mesh.shape["sub"]),
        mesh=mesh,
        in_specs=placed,
        out_specs=(P(split, None),) * 2 + (P(),) * 11,
        check_vma=False,
    )
```

```python
import functools

import jax
import jax.numpy as jnp
from jax import lax
from jax.experimental import pallas as pl
from jax.experimental.pallas import tpu as pltpu
from jax.sharding import PartitionSpec as P

F32 = jnp.float32
BF16 = jnp.bfloat16
EPS = 1e-05
G_local, G_edge, G_edge_back, G_grads = 1, 2, 2, 1


def mm(a, b):
    return jnp.dot(a, b, preferred_element_type=F32)


def mm_tn(a, b):
    return lax.dot_general(a, b, (((0,), (0,)), ((), ())), preferred_element_type=F32)


def mm_nt(a, b):
    return lax.dot_general(a, b, (((1,), (1,)), ((), ())), preferred_element_type=F32)


def rsum(v):
    return jnp.sum(v, axis=0, keepdims=True)


def lmean(v):
    return jnp.mean(v, axis=-1, keepdims=True)


def remote(src, dst, send_sem, recv_sem, device):
    return pltpu.make_async_remote_copy(
        src_ref=src,
        dst_ref=dst,
        send_sem=send_sem,
        recv_sem=recv_sem,
        device_id=device,
        device_id_type=pl.DeviceIdType.MESH,
    )


def as_column(row):
    width = row.shape[1]
    eye = lax.broadcasted_iota(jnp.int32, (width, width), 0) == lax.broadcasted_iota(
        jnp.int32, (width, width), 1
    )
    return jnp.sum(jnp.where(eye, row.astype(F32), 0.0), axis=1, keepdims=True)


def grouped(tiles, group, body):
    def several(t, carry):
        for i in range(group):
            body(t * group + i)
        return carry

    lax.fori_loop(0, tiles // group, several, 0)


def silu_parts(x):
    sig = 0.5 * jnp.tanh(0.5 * x) + 0.5
    return x * sig, sig * (1.0 + x * (1.0 - sig))


def kernel(dims, *refs):
    nd, ns, layers, n, e, sr, D, te, r2 = dims
    (nodes, edges, snd, rcv, live, flags, send,
     w1, b1, w2, o1, g1, wn, nb, wn2, no, ng, wo, gout,
     out_l, out_g, out_q, out_b,
     ohs, ohst, ohr, ohrt, ohx, ohxt, fcol,
     c_w1, c_w2, c_wn, c_wn2, c_wo,
     joined, act, ds1, xhat, rstd, estate, summed,
     nin, hid, dsn, nxhat, nrstd, lat,
     sent, halo, hgrad, ret,
     dedge, dp1, dp2, dext, dsh, glat, acc1, acc2, bacc,
     flat, r1, f2, rr2, g3, g4, br1, bs1, br2,
     hs_s, hs_r, hb_s, hb_r, q1s, q1r, q2s, q2r, q3s, q3r, q4s, q4r, bq1s, bq1r, bq2s, bq2r,
     ) = refs
    d = lax.axis_index("dom")
    s = lax.axis_index("sub")
    low, high = sr // 6, sr // 3
    c1 = nd * r2
    tiles = e // te
    hid_rows = w2.shape[1]
    k1 = w1.shape[1]
    kn = wn.shape[1]

    halo[...] = jnp.zeros_like(halo)
    ret[...] = jnp.zeros_like(ret)

    barrier = pltpu.get_barrier_semaphore()
    for k in range(1, ns):
        pl.semaphore_signal(barrier, inc=1, device_id=(d, lax.rem(s + k, ns)),
                            device_id_type=pl.DeviceIdType.MESH)
    for k in range(1, nd):
        pl.semaphore_signal(barrier, inc=1, device_id=(lax.rem(d + k, nd), s),
                            device_id_type=pl.DeviceIdType.MESH)
    pl.semaphore_wait(barrier, ns - 1 + nd - 1)

    S_rows = [(low, low), (0, low), (2 * low + high, high), (2 * low, high)]
    H_rows = [(0, low), (low, low), (2 * low, high), (2 * low + high, high)]
    has_next = [s < ns - 1, s > 0, d < nd - 1, d > 0]
    has_prev = [s > 0, s < ns - 1, d > 0, d < nd - 1]
    nxt = [(d, jnp.minimum(s + 1, ns - 1)), (d, jnp.maximum(s - 1, 0)),
           (jnp.minimum(d + 1, nd - 1), s), (jnp.maximum(d - 1, 0), s)]
    prv = [nxt[1], nxt[0], nxt[3], nxt[2]]

    def part(ref, layer, rows):
        return ref.at[layer, pl.ds(rows[0], rows[1])]

    def halo_copy(layer, i):
        return remote(part(sent, layer, S_rows[i]), part(halo, layer, H_rows[i]),
                      hs_s.at[layer, i], hs_r.at[layer, i], nxt[i])

    def back_copy(layer, i):
        return remote(part(hgrad, layer, H_rows[i]), part(ret, layer, S_rows[i]),
                      hb_s.at[layer, i], hb_r.at[layer, i], prv[i])

    def start_moves(make, layer, sends):
        for i in range(4):
            @pl.when(sends[i])
            def _(i=i):
                make(layer, i).start()

    def wait_moves(make, layer, sends, recvs):
        for i in range(4):
            @pl.when(recvs[i])
            def _(i=i):
                make(layer, i).wait_recv()
        for i in range(4):
            @pl.when(sends[i])
            def _(i=i):
                make(layer, i).wait_send()

    def build(ids, count, oh, oht, mask):
        width = oh.shape[1]
        short = jnp.int16
        down = lax.broadcasted_iota(jnp.int32, (width, 128), 0).astype(short)
        across = lax.broadcasted_iota(jnp.int32, (16, width), 1).astype(short)
        across = jnp.concatenate([across] * 8, axis=0)

        def hit(a, b):
            return jnp.where(a == b, jnp.ones(a.shape, BF16), jnp.zeros(a.shape, BF16))

        def body(r, carry):
            row = ids[pl.ds(r, 1), :]
            if mask is not None:
                row = jnp.where(mask[pl.ds(r, 1), :] > 0, row, -1)
            at = pl.multiple_of(r * 128, 128)
            wide = jnp.broadcast_to(row, (16, 128)).astype(short)
            oht[:, pl.ds(at, 128)] = hit(down, jnp.concatenate([wide] * (width // 16), axis=0))
            col = jnp.broadcast_to(as_column(row).astype(jnp.int32), (128, 128)).astype(short)
            oh[pl.ds(at, 128), :] = hit(across, jnp.concatenate([col] * (width // 128), axis=1))
            return carry

        lax.fori_loop(0, count // 128, body, 0)

    build(send, sr, ohx, ohxt, None)

    lat[...] = nodes[...].astype(F32)

    def start_layer(layer):
        own = lat[...].astype(BF16)
        nin[layer, :, 0:D] = own
        sent[layer] = mm(ohx[...], own).astype(BF16)
        start_moves(halo_copy, layer, has_next)

    start_layer(0)
    build(snd, e, ohs, ohst, None)
    build(rcv, e, ohr, ohrt, live)

    def flag_body(r, carry):
        at = pl.multiple_of(r * 128, 128)
        fcol[pl.ds(at, 128), :] = as_column(flags[pl.ds(r, 1), :])
        return carry

    lax.fori_loop(0, n // 128, flag_body, 0)
    for layer in range(layers):
        c_w1[layer] = w1[layer].astype(BF16)
        c_w2[layer] = w2[layer].astype(BF16)
        c_wn[layer] = wn[layer].astype(BF16)
        c_wn2[layer] = wn2[layer].astype(BF16)
        c_wo[layer] = wo[layer].astype(BF16)
    bacc[...] = jnp.zeros_like(bacc)
    estate[...] = edges[...].astype(F32)
    pad = flat.shape[1] - (k1 + hid_rows + kn + 2 * D)
    if pad:
        for layer in range(layers):
            flat[layer, pl.ds(k1 + hid_rows + kn + 2 * D, pad), :] = jnp.zeros((pad, D), BF16)

    for layer in range(layers):
        own = nin[layer, :, 0:D]

        def local(t, layer=layer):
            rows = pl.ds(pl.multiple_of(t * te, te), te)
            own = nin[layer, :, 0:D]
            joined[layer, rows, 0:D] = estate[rows, :].astype(BF16)
            joined[layer, rows, D:2 * D] = mm(ohs[rows, 0:n], own).astype(BF16)
            joined[layer, rows, 2 * D:3 * D] = mm(ohr[rows, :], own).astype(BF16)

        grouped(tiles, G_local, local)
        summed[...] = jnp.zeros_like(summed)
        wait_moves(halo_copy, layer, has_next, has_prev)

        def edge(t, layer=layer):
            rows = pl.ds(pl.multiple_of(t * te, te), te)
            far = mm(ohs[rows, n:], halo[layer])
            xs = (joined[layer, rows, D:2 * D].astype(F32) + far).astype(BF16)
            joined[layer, rows, D:2 * D] = xs
            pre = mm(joined[layer, rows, :], c_w1[layer]) + b1[pl.ds(layer, 1), :]
            a, da = silu_parts(pre)
            a = a.astype(BF16)
            act[layer, rows, :] = a
            ds1[layer, rows, :] = da
            two = mm(a, c_w2[layer]) + o1[pl.ds(layer, 1), :]
            cen = two - lmean(two)
            rs = lax.rsqrt(lmean(cen * cen) + EPS)
            xh = cen * rs
            xhat[layer, rows, :] = xh
            rstd[layer, rows, :] = rs
            msg = g1[pl.ds(layer, 1), :] * xh
            estate[rows, :] += msg
            summed[...] += mm(ohrt[:, rows], msg.astype(BF16))

        grouped(tiles, G_edge, edge)

        sh = summed[...].astype(BF16)
        nin[layer, :, D:2 * D] = sh
        pre = mm(nin[layer], c_wn[layer]) + nb[pl.ds(layer, 1), :]
        a, da = silu_parts(pre)
        a = a.astype(BF16)
        hid[layer] = a
        dsn[layer] = da
        two = mm(a, c_wn2[layer]) + no[pl.ds(layer, 1), :]
        cen = two - lmean(two)
        rs = lax.rsqrt(lmean(cen * cen) + EPS)
        xh = cen * rs
        nxhat[layer] = xh
        nrstd[layer] = rs
        lat[...] = lat[...] + ng[pl.ds(layer, 1), :] * xh + fcol[...] * mm(sh, c_wo[layer])
        if layer + 1 < layers:
            start_layer(layer + 1)
    out_l[...] = lat[...]

    def s1(layer, k):
        peer = lax.rem(s + k, ns)
        return remote(flat.at[layer, pl.ds(pl.multiple_of(peer * c1, 16), c1)], r1.at[layer, s],
                      q1s.at[layer, k], q1r.at[layer, k], (d, peer))

    def s2(layer, k):
        peer = lax.rem(d + k, nd)
        return remote(f2.at[layer, pl.ds(pl.multiple_of(peer * r2, 16), r2)], rr2.at[layer, d],
                      q2s.at[layer, k], q2r.at[layer, k], (peer, s))

    def s3(layer, k):
        peer = lax.rem(d + k, nd)
        mine = g3.at[layer, pl.ds(pl.multiple_of(d * r2, 16), r2)]
        return remote(mine, mine, q3s.at[layer, k], q3r.at[layer, k], (peer, s))

    def s4(layer, k):
        peer = lax.rem(s + k, ns)
        return remote(g3.at[layer], g4.at[layer, pl.ds(pl.multiple_of(s * c1, 16), c1)],
                      q4s.at[layer, k], q4r.at[layer, k], (d, peer))

    def bias1(layer, k):
        return remote(bacc, br1.at[s], bq1s.at[k], bq1r.at[k], (d, lax.rem(s + k, ns)))

    def bias2(layer, k):
        return remote(bs1, br2.at[d], bq2s.at[k], bq2r.at[k], (lax.rem(d + k, nd), s))

    def start_all(make, layer, count):
        for k in range(1, count):
            make(layer, k).start()

    def wait_all(make, layer, count):
        for k in range(1, count):
            make(layer, k).wait_recv()
        for k in range(1, count):
            make(layer, k).wait_send()

    def stage1(layer):
        start_all(s1, layer, ns)

    def stage2(layer):
        r1[layer, s] = flat[layer, pl.ds(pl.multiple_of(s * c1, 16), c1), :]
        wait_all(s1, layer, ns)
        total = r1[layer, 0].astype(F32)
        for j in range(1, ns):
            total = total + r1[layer, j].astype(F32)
        f2[layer] = total.astype(BF16)
        start_all(s2, layer, nd)

    def stage3(layer):
        rr2[layer, d] = f2[layer, pl.ds(pl.multiple_of(d * r2, 16), r2), :]
        wait_all(s2, layer, nd)
        total = rr2[layer, 0].astype(F32)
        for j in range(1, nd):
            total = total + rr2[layer, j].astype(F32)
        g3[layer, pl.ds(pl.multiple_of(d * r2, 16), r2), :] = total.astype(BF16)
        start_all(s3, layer, nd)

    def stage4(layer):
        wait_all(s3, layer, nd)
        start_all(s4, layer, ns)
        g4[layer, pl.ds(pl.multiple_of(s * c1, 16), c1), :] = g3[layer]

    def stage5(layer):
        wait_all(s4, layer, ns)
        out_q[layer] = g4[layer]

    def norm_back(dxh, xh, rs):
        return rs * (dxh - lmean(dxh) - xh * lmean(dxh * xh))

    glat[...] = gout[...]
    dedge[...] = jnp.zeros_like(dedge)
    for layer in reversed(range(layers)):
        row = layer * 6
        g = glat[...]
        xh = nxhat[layer]
        bacc[pl.ds(row + 5, 1), :] = rsum(g * xh)
        dtwo = norm_back(g * ng[pl.ds(layer, 1), :], xh, nrstd[layer])
        bacc[pl.ds(row + 4, 1), :] = rsum(dtwo)
        dtwo = dtwo.astype(BF16)
        dh = mm_nt(dtwo, c_wn2[layer]).astype(BF16).astype(F32)
        dpre = dh * dsn[layer]
        bacc[pl.ds(row + 3, 1), :] = rsum(dpre)
        dpre = dpre.astype(BF16)
        dout = (fcol[...] * g).astype(BF16)
        dnin = mm_nt(dpre, c_wn[layer])
        dsum = dnin[:, D:].astype(BF16).astype(F32) + mm_nt(dout, c_wo[layer]).astype(BF16).astype(F32)
        dsh[...] = dsum.astype(BF16)
        dext[...] = jnp.zeros_like(dext)
        glat[...] = g + dnin[:, :D]

        def edge_back(t, layer=layer, row=row):
            rows = pl.ds(pl.multiple_of(t * te, te), te)
            dmsg = dedge[rows, :] + mm(ohr[rows, :], dsh[...])
            xh = xhat[layer, rows, :]
            bacc[pl.ds(row + 2, 1), :] += rsum(dmsg * xh)
            dtwo = norm_back(dmsg * g1[pl.ds(layer, 1), :], xh, rstd[layer, rows, :])
            bacc[pl.ds(row + 1, 1), :] += rsum(dtwo)
            dtwo = dtwo.astype(BF16)
            dp2[rows, :] = dtwo
            da = mm_nt(dtwo, c_w2[layer]).astype(BF16).astype(F32)
            dpre = da * ds1[layer, rows, :]
            bacc[pl.ds(row, 1), :] += rsum(dpre)
            dpre = dpre.astype(BF16)
            dp1[rows, :] = dpre
            dj = mm_nt(dpre, c_w1[layer]).astype(BF16)
            dext[...] += mm(ohst[:, rows], dj[:, D:2 * D])
            glat[...] += mm(ohrt[:, rows], dj[:, 2 * D:])
            if layer > 0:
                dedge[rows, :] += dj[:, 0:D].astype(F32)

        grouped(tiles, G_edge_back, edge_back)
        hgrad[layer] = dext[n:, :].astype(BF16)
        start_moves(back_copy, layer, has_prev)

        acc1[...] = jnp.zeros_like(acc1)
        acc2[...] = jnp.zeros_like(acc2)

        def grads(t, layer=layer):
            rows = pl.ds(pl.multiple_of(t * te, te), te)
            acc1[...] += mm_tn(joined[layer, rows, :], dp1[rows, :])
            acc2[...] += mm_tn(act[layer, rows, :], dp2[rows, :])

        grouped(tiles, G_grads, grads)
        at = 0
        for value in (acc1[...], acc2[...], mm_tn(nin[layer], dpre),
                      mm_tn(hid[layer], dtwo), mm_tn(nin[layer, :, D:2 * D], dout)):
            count = value.shape[0]
            flat[layer, pl.ds(at, count), :] = value.astype(BF16)
            at += count
        stage1(layer)
        if layer == 0:
            start_all(bias1, 0, ns)
        if layer + 1 < layers:
            stage2(layer + 1)
        if layer + 2 < layers:
            stage4(layer + 2)
        glat[...] += dext[0:n, :]
        wait_moves(back_copy, layer, has_prev, has_next)
        glat[...] += mm(ohxt[...], ret[layer])
        if layer + 1 < layers:
            stage3(layer + 1)
        if layer + 2 < layers:
            stage5(layer + 2)
    out_g[...] = glat[...]

    stage2(0)
    br1[s] = bacc[...]
    wait_all(bias1, 0, ns)
    total = br1[0]
    for j in range(1, ns):
        total = total + br1[j]
    bs1[...] = total
    start_all(bias2, 0, nd)
    if layers > 1:
        stage4(1)
    stage3(0)
    br2[d] = bs1[...]
    wait_all(bias2, 0, nd)
    total = br2[0]
    for j in range(1, nd):
        total = total + br2[j]
    out_b[...] = total
    stage4(0)
    if layers > 1:
        stage5(1)
    stage5(0)


def finish(layers, lat, glat, grads, sums, out_l, out_g, *outs):
    q_w1, q_b1, q_w2, q_o1, q_g1, q_wn, q_nb, q_wn2, q_no, q_ng, q_wo = outs
    out_l[...] = lat[...]
    out_g[...] = glat[...]
    at = 0
    for out in (q_w1, q_w2, q_wn, q_wn2, q_wo):
        count = out.shape[1]
        for layer in range(layers):
            out[layer] = grads[layer, pl.ds(at, count), :].astype(F32)
        at += count
    for layer in range(layers):
        for i, out in enumerate((q_b1, q_o1, q_g1, q_nb, q_no, q_ng)):
            out[pl.ds(layer, 1), :] = sums[pl.ds(layer * 6 + i, 1), :]


def on_device(nd, ns, nodes, edges, senders, receivers, edge_live, outlet_flags, send_rows, *rest):
    weights, grad_out = rest[:-1], rest[-1]
    n, D = nodes.shape
    e = edges.shape[0]
    sr = send_rows.shape[0]
    layers = weights[0].shape[0]
    te = min(1024, e)
    grad_rows = sum(w.shape[1] for w in weights if w.ndim == 3)
    r2 = pl.cdiv(grad_rows, ns * nd * 16) * 16
    c1 = nd * r2
    total = ns * c1
    brows = pl.cdiv(6 * layers, 8) * 8
    ext = n + sr
    dims = (nd, ns, layers, n, e, sr, D, te, r2)
    V = pltpu.VMEM
    scratch = [
        V((e, ext), BF16), V((ext, e), BF16), V((e, n), BF16), V((n, e), BF16),
        V((sr, n), BF16), V((n, sr), BF16), V((n, 1), F32),
        V(weights[0].shape, BF16), V(weights[2].shape, BF16), V(weights[5].shape, BF16),
        V(weights[7].shape, BF16), V(weights[10].shape, BF16),
        V((layers, e, 3 * D), BF16), V((layers, e, D), BF16), V((layers, e, D), F32),
        V((layers, e, D), F32), V((layers, e, 1), F32), V((e, D), F32), V((n, D), F32),
        V((layers, n, 2 * D), BF16), V((layers, n, D), BF16), V((layers, n, D), F32),
        V((layers, n, D), F32), V((layers, n, 1), F32), V((n, D), F32),
        V((layers, sr, D), BF16), V((layers, sr, D), BF16), V((layers, sr, D), BF16),
        V((layers, sr, D), BF16),
        V((e, D), F32), V((e, D), BF16), V((e, D), BF16), V((ext, D), F32), V((n, D), BF16),
        V((n, D), F32), V((3 * D, D), F32), V((D, D), F32), V((brows, D), F32),
        V((layers, total, D), BF16), V((layers, ns, c1, D), BF16), V((layers, c1, D), BF16),
        V((layers, nd, r2, D), BF16), V((layers, c1, D), BF16), V((layers, total, D), BF16),
        V((ns, brows, D), F32), V((brows, D), F32), V((nd, brows, D), F32),
    ]
    sem = pltpu.SemaphoreType.DMA
    scratch += [sem((layers, 4))] * 4
    scratch += [sem((layers, ns))] * 2 + [sem((layers, nd))] * 4 + [sem((layers, ns))] * 2
    scratch += [sem((ns,))] * 2 + [sem((nd,))] * 2
    shapes = [jax.ShapeDtypeStruct((n, D), F32)] * 2 + [
        jax.ShapeDtypeStruct(w.shape, F32) for w in weights
    ]
    vmem = pl.BlockSpec(memory_space=pltpu.VMEM)
    rows = lambda v: v.reshape(-1, 128)
    args = (nodes, edges, rows(senders), rows(receivers), rows(edge_live), rows(outlet_flags),
            rows(send_rows), *weights, grad_out)
    mid = shapes[:2] + [
        jax.ShapeDtypeStruct((layers, total, D), BF16),
        jax.ShapeDtypeStruct((brows, D), F32),
    ]
    found = pl.pallas_call(
        functools.partial(kernel, dims),
        out_shape=mid,
        in_specs=[vmem] * len(args),
        out_specs=[vmem] * len(mid),
        scratch_shapes=scratch,
        compiler_params=pltpu.CompilerParams(
            collective_id=0, has_side_effects=True, vmem_limit_bytes=60 * 1024 * 1024
        ),
    )(*args)
    return tuple(pl.pallas_call(
        functools.partial(finish, layers),
        out_shape=shapes,
        in_specs=[vmem] * len(mid),
        out_specs=[vmem] * len(shapes),
    )(*found))


def solution(mesh):
    split = ("dom", "sub")
    placed = (P(split, None),) * 2 + (P(split),) * 5 + (P(),) * 11 + (P(split, None),)
    return jax.shard_map(
        functools.partial(on_device, mesh.shape["dom"], mesh.shape["sub"]),
        mesh=mesh,
        in_specs=placed,
        out_specs=(P(split, None),) * 2 + (P(),) * 11,
        check_vma=False,
    )
```

```python
import functools

import jax
import jax.numpy as jnp
from jax import lax
from jax.experimental import pallas as pl
from jax.experimental.pallas import tpu as pltpu
from jax.sharding import PartitionSpec as P

F32 = jnp.float32
BF16 = jnp.bfloat16
EPS = 1e-05
G_local, G_edge, G_edge_back, G_grads = 2, 2, 2, 2


def mm(a, b):
    return jnp.dot(a, b, preferred_element_type=F32)


def mm_tn(a, b):
    return lax.dot_general(a, b, (((0,), (0,)), ((), ())), preferred_element_type=F32)


def mm_nt(a, b):
    return lax.dot_general(a, b, (((1,), (1,)), ((), ())), preferred_element_type=F32)


def rsum(v):
    return jnp.sum(v, axis=0, keepdims=True)


def lmean(v):
    return jnp.mean(v, axis=-1, keepdims=True)


def remote(src, dst, send_sem, recv_sem, device):
    return pltpu.make_async_remote_copy(
        src_ref=src,
        dst_ref=dst,
        send_sem=send_sem,
        recv_sem=recv_sem,
        device_id=device,
        device_id_type=pl.DeviceIdType.MESH,
    )


def as_column(row):
    width = row.shape[1]
    eye = lax.broadcasted_iota(jnp.int32, (width, width), 0) == lax.broadcasted_iota(
        jnp.int32, (width, width), 1
    )
    return jnp.sum(jnp.where(eye, row.astype(F32), 0.0), axis=1, keepdims=True)


def grouped(tiles, group, body):
    def several(t, carry):
        for i in range(group):
            body(t * group + i)
        return carry

    lax.fori_loop(0, tiles // group, several, 0)


def silu_parts(x):
    sig = 0.5 * jnp.tanh(0.5 * x) + 0.5
    return x * sig, sig * (1.0 + x * (1.0 - sig))


def kernel(dims, *refs):
    nd, ns, layers, n, e, sr, D, te, r2 = dims
    (nodes, edges, snd, rcv, live, flags, send,
     w1, b1, w2, o1, g1, wn, nb, wn2, no, ng, wo, gout,
     out_l, out_g, out_q, out_b,
     ohs, ohst, ohr, ohrt, ohx, ohxt, fcol,
     c_w1, c_w2, c_wn, c_wn2, c_wo,
     joined, act, ds1, xhat, rstd, estate, summed,
     nin, hid, dsn, nxhat, nrstd, lat,
     sent, halo, hgrad, ret,
     dedge, dp1, dp2, dext, dsh, glat, acc1, acc2, bacc,
     flat, r1, f2, rr2, g3, g4, br1, bs1, br2,
     hs_s, hs_r, hb_s, hb_r, q1s, q1r, q2s, q2r, q3s, q3r, q4s, q4r, bq1s, bq1r, bq2s, bq2r,
     ) = refs
    d = lax.axis_index("dom")
    s = lax.axis_index("sub")
    low, high = sr // 6, sr // 3
    c1 = nd * r2
    tiles = e // te
    hid_rows = w2.shape[1]
    k1 = w1.shape[1]
    kn = wn.shape[1]

    halo[...] = jnp.zeros_like(halo)
    ret[...] = jnp.zeros_like(ret)

    barrier = pltpu.get_barrier_semaphore()
    for k in range(1, ns):
        pl.semaphore_signal(barrier, inc=1, device_id=(d, lax.rem(s + k, ns)),
                            device_id_type=pl.DeviceIdType.MESH)
    for k in range(1, nd):
        pl.semaphore_signal(barrier, inc=1, device_id=(lax.rem(d + k, nd), s),
                            device_id_type=pl.DeviceIdType.MESH)
    pl.semaphore_wait(barrier, ns - 1 + nd - 1)

    S_rows = [(low, low), (0, low), (2 * low + high, high), (2 * low, high)]
    H_rows = [(0, low), (low, low), (2 * low, high), (2 * low + high, high)]
    has_next = [s < ns - 1, s > 0, d < nd - 1, d > 0]
    has_prev = [s > 0, s < ns - 1, d > 0, d < nd - 1]
    nxt = [(d, jnp.minimum(s + 1, ns - 1)), (d, jnp.maximum(s - 1, 0)),
           (jnp.minimum(d + 1, nd - 1), s), (jnp.maximum(d - 1, 0), s)]
    prv = [nxt[1], nxt[0], nxt[3], nxt[2]]

    def part(ref, layer, rows):
        return ref.at[layer, pl.ds(rows[0], rows[1])]

    def halo_copy(layer, i):
        return remote(part(sent, layer, S_rows[i]), part(halo, layer, H_rows[i]),
                      hs_s.at[layer, i], hs_r.at[layer, i], nxt[i])

    def back_copy(layer, i):
        return remote(part(hgrad, layer, H_rows[i]), part(ret, layer, S_rows[i]),
                      hb_s.at[layer, i], hb_r.at[layer, i], prv[i])

    def start_moves(make, layer, sends):
        for i in range(4):
            @pl.when(sends[i])
            def _(i=i):
                make(layer, i).start()

    def wait_moves(make, layer, sends, recvs):
        for i in range(4):
            @pl.when(recvs[i])
            def _(i=i):
                make(layer, i).wait_recv()
        for i in range(4):
            @pl.when(sends[i])
            def _(i=i):
                make(layer, i).wait_send()

    def build(ids, count, oh, oht, mask):
        width = oh.shape[1]
        short = jnp.int16
        down = lax.broadcasted_iota(jnp.int32, (width, 128), 0).astype(short)
        across = lax.broadcasted_iota(jnp.int32, (16, width), 1).astype(short)
        across = jnp.concatenate([across] * 8, axis=0)

        def hit(a, b):
            return jnp.where(a == b, jnp.ones(a.shape, BF16), jnp.zeros(a.shape, BF16))

        def body(r, carry):
            row = ids[pl.ds(r, 1), :]
            if mask is not None:
                row = jnp.where(mask[pl.ds(r, 1), :] > 0, row, -1)
            at = pl.multiple_of(r * 128, 128)
            wide = jnp.broadcast_to(row, (16, 128)).astype(short)
            oht[:, pl.ds(at, 128)] = hit(down, jnp.concatenate([wide] * (width // 16), axis=0))
            col = jnp.broadcast_to(as_column(row).astype(jnp.int32), (128, 128)).astype(short)
            oh[pl.ds(at, 128), :] = hit(across, jnp.concatenate([col] * (width // 128), axis=1))
            return carry

        lax.fori_loop(0, count // 128, body, 0)

    build(send, sr, ohx, ohxt, None)

    lat[...] = nodes[...].astype(F32)

    def start_layer(layer):
        own = lat[...].astype(BF16)
        nin[layer, :, 0:D] = own
        sent[layer] = mm(ohx[...], own).astype(BF16)
        start_moves(halo_copy, layer, has_next)

    start_layer(0)
    build(snd, e, ohs, ohst, None)
    build(rcv, e, ohr, ohrt, live)

    def flag_body(r, carry):
        at = pl.multiple_of(r * 128, 128)
        fcol[pl.ds(at, 128), :] = as_column(flags[pl.ds(r, 1), :])
        return carry

    lax.fori_loop(0, n // 128, flag_body, 0)
    for layer in range(layers):
        c_w1[layer] = w1[layer].astype(BF16)
        c_w2[layer] = w2[layer].astype(BF16)
        c_wn[layer] = wn[layer].astype(BF16)
        c_wn2[layer] = wn2[layer].astype(BF16)
        c_wo[layer] = wo[layer].astype(BF16)
    bacc[...] = jnp.zeros_like(bacc)
    estate[...] = edges[...].astype(F32)
    pad = flat.shape[1] - (k1 + hid_rows + kn + 2 * D)
    if pad:
        for layer in range(layers):
            flat[layer, pl.ds(k1 + hid_rows + kn + 2 * D, pad), :] = jnp.zeros((pad, D), BF16)

    for layer in range(layers):
        own = nin[layer, :, 0:D]

        def local(t, layer=layer):
            rows = pl.ds(pl.multiple_of(t * te, te), te)
            own = nin[layer, :, 0:D]
            joined[layer, rows, 0:D] = estate[rows, :].astype(BF16)
            joined[layer, rows, D:2 * D] = mm(ohs[rows, 0:n], own).astype(BF16)
            joined[layer, rows, 2 * D:3 * D] = mm(ohr[rows, :], own).astype(BF16)

        grouped(tiles, G_local, local)
        summed[...] = jnp.zeros_like(summed)
        wait_moves(halo_copy, layer, has_next, has_prev)

        def edge(t, layer=layer):
            rows = pl.ds(pl.multiple_of(t * te, te), te)
            far = mm(ohs[rows, n:], halo[layer])
            xs = (joined[layer, rows, D:2 * D].astype(F32) + far).astype(BF16)
            joined[layer, rows, D:2 * D] = xs
            pre = mm(joined[layer, rows, :], c_w1[layer]) + b1[pl.ds(layer, 1), :]
            a, da = silu_parts(pre)
            a = a.astype(BF16)
            act[layer, rows, :] = a
            ds1[layer, rows, :] = da
            two = mm(a, c_w2[layer]) + o1[pl.ds(layer, 1), :]
            cen = two - lmean(two)
            rs = lax.rsqrt(lmean(cen * cen) + EPS)
            xh = cen * rs
            xhat[layer, rows, :] = xh
            rstd[layer, rows, :] = rs
            msg = g1[pl.ds(layer, 1), :] * xh
            estate[rows, :] += msg
            summed[...] += mm(ohrt[:, rows], msg.astype(BF16))

        grouped(tiles, G_edge, edge)

        sh = summed[...].astype(BF16)
        nin[layer, :, D:2 * D] = sh
        pre = mm(nin[layer], c_wn[layer]) + nb[pl.ds(layer, 1), :]
        a, da = silu_parts(pre)
        a = a.astype(BF16)
        hid[layer] = a
        dsn[layer] = da
        two = mm(a, c_wn2[layer]) + no[pl.ds(layer, 1), :]
        cen = two - lmean(two)
        rs = lax.rsqrt(lmean(cen * cen) + EPS)
        xh = cen * rs
        nxhat[layer] = xh
        nrstd[layer] = rs
        lat[...] = lat[...] + ng[pl.ds(layer, 1), :] * xh + fcol[...] * mm(sh, c_wo[layer])
        if layer + 1 < layers:
            start_layer(layer + 1)
    out_l[...] = lat[...]

    def s1(layer, k):
        peer = lax.rem(s + k, ns)
        return remote(flat.at[layer, pl.ds(pl.multiple_of(peer * c1, 16), c1)], r1.at[layer, s],
                      q1s.at[layer, k], q1r.at[layer, k], (d, peer))

    def s2(layer, k):
        peer = lax.rem(d + k, nd)
        return remote(f2.at[layer, pl.ds(pl.multiple_of(peer * r2, 16), r2)], rr2.at[layer, d],
                      q2s.at[layer, k], q2r.at[layer, k], (peer, s))

    def s3(layer, k):
        peer = lax.rem(d + k, nd)
        mine = g3.at[layer, pl.ds(pl.multiple_of(d * r2, 16), r2)]
        return remote(mine, mine, q3s.at[layer, k], q3r.at[layer, k], (peer, s))

    def s4(layer, k):
        peer = lax.rem(s + k, ns)
        return remote(g3.at[layer], g4.at[layer, pl.ds(pl.multiple_of(s * c1, 16), c1)],
                      q4s.at[layer, k], q4r.at[layer, k], (d, peer))

    def bias1(layer, k):
        return remote(bacc, br1.at[s], bq1s.at[k], bq1r.at[k], (d, lax.rem(s + k, ns)))

    def bias2(layer, k):
        return remote(bs1, br2.at[d], bq2s.at[k], bq2r.at[k], (lax.rem(d + k, nd), s))

    def start_all(make, layer, count):
        for k in range(1, count):
            make(layer, k).start()

    def wait_all(make, layer, count):
        for k in range(1, count):
            make(layer, k).wait_recv()
        for k in range(1, count):
            make(layer, k).wait_send()

    def stage1(layer):
        start_all(s1, layer, ns)

    def stage2(layer):
        r1[layer, s] = flat[layer, pl.ds(pl.multiple_of(s * c1, 16), c1), :]
        wait_all(s1, layer, ns)
        total = r1[layer, 0].astype(F32)
        for j in range(1, ns):
            total = total + r1[layer, j].astype(F32)
        f2[layer] = total.astype(BF16)
        start_all(s2, layer, nd)

    def stage3(layer):
        rr2[layer, d] = f2[layer, pl.ds(pl.multiple_of(d * r2, 16), r2), :]
        wait_all(s2, layer, nd)
        total = rr2[layer, 0].astype(F32)
        for j in range(1, nd):
            total = total + rr2[layer, j].astype(F32)
        g3[layer, pl.ds(pl.multiple_of(d * r2, 16), r2), :] = total.astype(BF16)
        start_all(s3, layer, nd)

    def stage4(layer):
        wait_all(s3, layer, nd)
        start_all(s4, layer, ns)
        g4[layer, pl.ds(pl.multiple_of(s * c1, 16), c1), :] = g3[layer]

    def stage5(layer):
        wait_all(s4, layer, ns)
        out_q[layer] = g4[layer]

    def norm_back(dxh, xh, rs):
        return rs * (dxh - lmean(dxh) - xh * lmean(dxh * xh))

    glat[...] = gout[...]
    dedge[...] = jnp.zeros_like(dedge)
    for layer in reversed(range(layers)):
        row = layer * 6
        g = glat[...]
        xh = nxhat[layer]
        bacc[pl.ds(row + 5, 1), :] = rsum(g * xh)
        dtwo = norm_back(g * ng[pl.ds(layer, 1), :], xh, nrstd[layer])
        bacc[pl.ds(row + 4, 1), :] = rsum(dtwo)
        dtwo = dtwo.astype(BF16)
        dh = mm_nt(dtwo, c_wn2[layer]).astype(BF16).astype(F32)
        dpre = dh * dsn[layer]
        bacc[pl.ds(row + 3, 1), :] = rsum(dpre)
        dpre = dpre.astype(BF16)
        dout = (fcol[...] * g).astype(BF16)
        dnin = mm_nt(dpre, c_wn[layer])
        dsum = dnin[:, D:].astype(BF16).astype(F32) + mm_nt(dout, c_wo[layer]).astype(BF16).astype(F32)
        dsh[...] = dsum.astype(BF16)
        dext[...] = jnp.zeros_like(dext)
        glat[...] = g + dnin[:, :D]

        def edge_back(t, layer=layer, row=row):
            rows = pl.ds(pl.multiple_of(t * te, te), te)
            dmsg = dedge[rows, :] + mm(ohr[rows, :], dsh[...])
            xh = xhat[layer, rows, :]
            bacc[pl.ds(row + 2, 1), :] += rsum(dmsg * xh)
            dtwo = norm_back(dmsg * g1[pl.ds(layer, 1), :], xh, rstd[layer, rows, :])
            bacc[pl.ds(row + 1, 1), :] += rsum(dtwo)
            dtwo = dtwo.astype(BF16)
            dp2[rows, :] = dtwo
            da = mm_nt(dtwo, c_w2[layer]).astype(BF16).astype(F32)
            dpre = da * ds1[layer, rows, :]
            bacc[pl.ds(row, 1), :] += rsum(dpre)
            dpre = dpre.astype(BF16)
            dp1[rows, :] = dpre
            dj = mm_nt(dpre, c_w1[layer, D:3 * D, :]).astype(BF16)
            dext[...] += mm(ohst[:, rows], dj[:, 0:D])
            glat[...] += mm(ohrt[:, rows], dj[:, D:2 * D])
            if layer > 0:
                dedge[rows, :] += mm_nt(dpre, c_w1[layer, 0:D, :]).astype(BF16).astype(F32)

        grouped(tiles, G_edge_back, edge_back)
        hgrad[layer] = dext[n:, :].astype(BF16)
        start_moves(back_copy, layer, has_prev)

        acc1[...] = jnp.zeros_like(acc1)
        acc2[...] = jnp.zeros_like(acc2)

        def grads(t, layer=layer):
            rows = pl.ds(pl.multiple_of(t * te, te), te)
            acc1[...] += mm_tn(joined[layer, rows, :], dp1[rows, :])
            acc2[...] += mm_tn(act[layer, rows, :], dp2[rows, :])

        grouped(tiles, G_grads, grads)
        at = 0
        for value in (acc1[...], acc2[...], mm_tn(nin[layer], dpre),
                      mm_tn(hid[layer], dtwo), mm_tn(nin[layer, :, D:2 * D], dout)):
            count = value.shape[0]
            flat[layer, pl.ds(at, count), :] = value.astype(BF16)
            at += count
        stage1(layer)
        if layer == 0:
            start_all(bias1, 0, ns)
        if layer + 1 < layers:
            stage2(layer + 1)
        if layer + 2 < layers:
            stage4(layer + 2)
        glat[...] += dext[0:n, :]
        wait_moves(back_copy, layer, has_prev, has_next)
        glat[...] += mm(ohxt[...], ret[layer])
        if layer + 1 < layers:
            stage3(layer + 1)
        if layer + 2 < layers:
            stage5(layer + 2)
    out_g[...] = glat[...]

    stage2(0)
    br1[s] = bacc[...]
    wait_all(bias1, 0, ns)
    total = br1[0]
    for j in range(1, ns):
        total = total + br1[j]
    bs1[...] = total
    start_all(bias2, 0, nd)
    if layers > 1:
        stage4(1)
    stage3(0)
    br2[d] = bs1[...]
    wait_all(bias2, 0, nd)
    total = br2[0]
    for j in range(1, nd):
        total = total + br2[j]
    out_b[...] = total
    stage4(0)
    if layers > 1:
        stage5(1)
    stage5(0)


def finish(layers, lat, glat, grads, sums, out_l, out_g, *outs):
    q_w1, q_b1, q_w2, q_o1, q_g1, q_wn, q_nb, q_wn2, q_no, q_ng, q_wo = outs
    out_l[...] = lat[...]
    out_g[...] = glat[...]
    at = 0
    for out in (q_w1, q_w2, q_wn, q_wn2, q_wo):
        count = out.shape[1]
        for layer in range(layers):
            out[layer] = grads[layer, pl.ds(at, count), :].astype(F32)
        at += count
    for layer in range(layers):
        for i, out in enumerate((q_b1, q_o1, q_g1, q_nb, q_no, q_ng)):
            out[pl.ds(layer, 1), :] = sums[pl.ds(layer * 6 + i, 1), :]


def on_device(nd, ns, nodes, edges, senders, receivers, edge_live, outlet_flags, send_rows, *rest):
    weights, grad_out = rest[:-1], rest[-1]
    n, D = nodes.shape
    e = edges.shape[0]
    sr = send_rows.shape[0]
    layers = weights[0].shape[0]
    te = min(1024, e)
    grad_rows = sum(w.shape[1] for w in weights if w.ndim == 3)
    r2 = pl.cdiv(grad_rows, ns * nd * 16) * 16
    c1 = nd * r2
    total = ns * c1
    brows = pl.cdiv(6 * layers, 8) * 8
    ext = n + sr
    dims = (nd, ns, layers, n, e, sr, D, te, r2)
    V = pltpu.VMEM
    scratch = [
        V((e, ext), BF16), V((ext, e), BF16), V((e, n), BF16), V((n, e), BF16),
        V((sr, n), BF16), V((n, sr), BF16), V((n, 1), F32),
        V(weights[0].shape, BF16), V(weights[2].shape, BF16), V(weights[5].shape, BF16),
        V(weights[7].shape, BF16), V(weights[10].shape, BF16),
        V((layers, e, 3 * D), BF16), V((layers, e, D), BF16), V((layers, e, D), F32),
        V((layers, e, D), F32), V((layers, e, 1), F32), V((e, D), F32), V((n, D), F32),
        V((layers, n, 2 * D), BF16), V((layers, n, D), BF16), V((layers, n, D), F32),
        V((layers, n, D), F32), V((layers, n, 1), F32), V((n, D), F32),
        V((layers, sr, D), BF16), V((layers, sr, D), BF16), V((layers, sr, D), BF16),
        V((layers, sr, D), BF16),
        V((e, D), F32), V((e, D), BF16), V((e, D), BF16), V((ext, D), F32), V((n, D), BF16),
        V((n, D), F32), V((3 * D, D), F32), V((D, D), F32), V((brows, D), F32),
        V((layers, total, D), BF16), V((layers, ns, c1, D), BF16), V((layers, c1, D), BF16),
        V((layers, nd, r2, D), BF16), V((layers, c1, D), BF16), V((layers, total, D), BF16),
        V((ns, brows, D), F32), V((brows, D), F32), V((nd, brows, D), F32),
    ]
    sem = pltpu.SemaphoreType.DMA
    scratch += [sem((layers, 4))] * 4
    scratch += [sem((layers, ns))] * 2 + [sem((layers, nd))] * 4 + [sem((layers, ns))] * 2
    scratch += [sem((ns,))] * 2 + [sem((nd,))] * 2
    shapes = [jax.ShapeDtypeStruct((n, D), F32)] * 2 + [
        jax.ShapeDtypeStruct(w.shape, F32) for w in weights
    ]
    vmem = pl.BlockSpec(memory_space=pltpu.VMEM)
    rows = lambda v: v.reshape(-1, 128)
    args = (nodes, edges, rows(senders), rows(receivers), rows(edge_live), rows(outlet_flags),
            rows(send_rows), *weights, grad_out)
    mid = shapes[:2] + [
        jax.ShapeDtypeStruct((layers, total, D), BF16),
        jax.ShapeDtypeStruct((brows, D), F32),
    ]
    found = pl.pallas_call(
        functools.partial(kernel, dims),
        out_shape=mid,
        in_specs=[vmem] * len(args),
        out_specs=[vmem] * len(mid),
        scratch_shapes=scratch,
        compiler_params=pltpu.CompilerParams(
            collective_id=0, has_side_effects=True, vmem_limit_bytes=60 * 1024 * 1024
        ),
    )(*args)
    return tuple(pl.pallas_call(
        functools.partial(finish, layers),
        out_shape=shapes,
        in_specs=[vmem] * len(mid),
        out_specs=[vmem] * len(shapes),
    )(*found))


def solution(mesh):
    split = ("dom", "sub")
    placed = (P(split, None),) * 2 + (P(split),) * 5 + (P(),) * 11 + (P(split, None),)
    return jax.shard_map(
        functools.partial(on_device, mesh.shape["dom"], mesh.shape["sub"]),
        mesh=mesh,
        in_specs=placed,
        out_specs=(P(split, None),) * 2 + (P(),) * 11,
        check_vma=False,
    )
```
